256 devices in a mesh: ctx: 32 (over y, z), head: 8 (over x, core).
Axes of the slice: x: 4, y: 4, z: 8, core: 2. Of those that a mesh axis runs over, the one named last changes fastest.
Arguments:
- queries: bfloat16 [32768, 4096], P('ctx', 'head'), may hold values from -6 to 6
- keys: bfloat16 [32768, 1024], P('ctx', 'head'), may hold values from -6 to 6
- values: bfloat16 [32768, 1024], P('ctx', 'head'), may hold values from -6 to 6
- block_masks: int32 [32, 256], P('head', 'ctx'), may hold values from 0 to 255
- residual: bfloat16 [32768, 4096], P(('ctx', 'head')), may hold values from -1.5 to 1.5
- norm_gain: bfloat16 [4096], replicated, may hold values from 0.099609375 to 1.8984375
Outputs:
- stream: bfloat16 [32768, 4096], P(('ctx', 'head'))
- normed: bfloat16 [32768, 4096], P(('ctx', 'head'))
The draws below stay inside these ranges and needn't reach their ends.
Inputs may be any that keep to these rules, and one draw needn't show every extreme that they name: Bit b of block_masks[h, i] says whether query block i of head h attends to block i XOR 2^b; it is read only where that block comes earlier, and bits from 8 up are zero.
All inputs are finite; a program needn't handle non-finite values.
Results may differ from the reference program's by a relative error of at most 0.0052.
Values may be sent and summed in bfloat16 or wider, within the bound.
No kernel may reach another device: no remote copies, remote signals or barrier semaphores. Data moves between devices by JAX's collectives and lax.ppermute only.
A program may use at most 64 MiB of HBM per device.

```python
import jax
import jax.numpy as jnp
from jax import lax

QH = 32
KVH = 8
DH = 128
BLOCK = 128
D = 4096
LEVELS = 8
SEQ = 32768
NB = 256


def drawn_pair(key):
    base = jax.random.fold_in(key, 7)
    key_query, key_key = jax.random.split(base, 2)
    queries = jnp.clip(jax.random.normal(key_query, (SEQ, QH * DH), jnp.float32), -6.0, 6.0)
    keys = jnp.clip(jax.random.normal(key_key, (SEQ, KVH * DH), jnp.float32), -6.0, 6.0)
    return (queries, keys)


def draw_queries(key, part):
    queries, _ = drawn_pair(key)
    return queries.astype(jnp.bfloat16)


def draw_keys(key, part):
    _, keys = drawn_pair(key)
    return keys.astype(jnp.bfloat16)


def touch_ends(drawn, rng, least, top_value):
    shape = drawn.shape
    place = [jax.random.randint(jax.random.fold_in(rng, axis), (), 0, shape[axis]) for axis in range(len(shape))]
    drawn = drawn.at[tuple(place)].set(least)
    longest = shape.index(max(shape))
    place[longest] = (place[longest] + 1) % shape[longest]
    return drawn.at[tuple(place)].set(top_value)


def shard_levels(own_key, dims, shards, least, high):
    gain = 1.0
    for dim, parts in shards:
        draws = jax.random.uniform(jax.random.fold_in(jax.random.fold_in(own_key, 6), dim), (parts,), jnp.float32, least / len(shards), high / len(shards))
        gain = gain * jnp.repeat(jnp.exp(draws), dims[dim] // parts).reshape((-1,) + (1,) * (len(dims) - 1 - dim))
    return gain


def gaussian(stream_key, shape, spread, reach, shards=(), held_as=jnp.bfloat16):
    array = spread * jax.random.normal(stream_key, shape, jnp.float32)
    if shards:
        array = array * shard_levels(stream_key, shape, shards, -0.22, 0.18)
    return jnp.clip(array, -reach, reach).astype(held_as)


def setup_inputs(seed: int = 0) -> dict:
    key_of = jax.random.split(jax.random.key(seed), 7)
    return {
        "queries": draw_queries(jax.random.fold_in(key_of[6], 71), 0),
        "keys": draw_keys(jax.random.fold_in(key_of[6], 71), 0),
        "values": gaussian(key_of[2], (SEQ, KVH * DH), 1.0, 6.0, ((0, 32), (1, 8))),
        "block_masks": touch_ends(jax.random.randint(key_of[3], (QH, NB), 0, 2 ** LEVELS), jax.random.fold_in(key_of[3], 1), 0, (2 ** LEVELS) - 1).astype(jnp.int32),
        "residual": gaussian(key_of[4], (SEQ, D), 0.1, 1.5, ((0, 256),)),
        "norm_gain": jnp.clip(1.0 + 0.18 * jax.random.normal(key_of[5], (D,), jnp.float32), 0.099609375, 1.8984375).astype(jnp.bfloat16),
    }


MASKED_SCORE = -1e+30
EPSILON = 1e-05

def split_upper(source, axis_at, stride):
    extent = source.shape
    length = extent[axis_at]
    folded = source.reshape(extent[:axis_at] + (length // (2 * stride), 2, stride) + extent[axis_at + 1:])
    low_part = lax.index_in_dim(folded, 0, axis_at + 1, keepdims=False)
    high_part = lax.index_in_dim(folded, 1, axis_at + 1, keepdims=False)
    flattened = extent[:axis_at] + (length // 2,) + extent[axis_at + 1:]
    return (low_part.reshape(flattened), high_part.reshape(flattened))

def join_halves(low_part, high_part, axis_at, stride):
    extent = low_part.shape
    length = extent[axis_at]
    folded = extent[:axis_at] + (length // stride, 1, stride) + extent[axis_at + 1:]
    stacked = jnp.concatenate([low_part.reshape(folded), high_part.reshape(folded)], axis=axis_at + 1)
    return stacked.reshape(extent[:axis_at] + (length * 2,) + extent[axis_at + 1:])

def round_weights(weights):
    rounded = lax.optimization_barrier(weights.astype(jnp.bfloat16))
    return rounded.astype(jnp.float32)

def reference(queries, keys, values, block_masks, residual, norm_gain):
    sequence = queries.shape[0]
    block_count = sequence // BLOCK
    levels = block_count.bit_length() - 1
    group_size = QH // KVH
    scaling = DH ** (-0.5)
    query_heads = queries.reshape(block_count, BLOCK, QH, DH).transpose(2, 0, 1, 3)
    key_heads = keys.reshape(block_count, BLOCK, KVH, DH).transpose(2, 0, 1, 3)
    value_heads = values.reshape(block_count, BLOCK, KVH, DH).transpose(2, 0, 1, 3)
    causal = lax.broadcasted_iota(jnp.int32, (BLOCK, BLOCK), 0) >= lax.broadcasted_iota(jnp.int32, (BLOCK, BLOCK), 1)

    def one_head(head_number):
        kv_head = head_number // group_size
        query_part = lax.dynamic_index_in_dim(query_heads, head_number, 0, keepdims=False).astype(jnp.float32)
        key_part = lax.dynamic_index_in_dim(key_heads, kv_head, 0, keepdims=False).astype(jnp.float32)
        value_part = lax.dynamic_index_in_dim(value_heads, kv_head, 0, keepdims=False).astype(jnp.float32)
        head_bits = lax.dynamic_index_in_dim(block_masks, head_number, 0, keepdims=False)
        diagonal = jnp.einsum('nqd,nkd->nqk', query_part, key_part) * scaling
        diagonal = jnp.where(causal[None], diagonal, MASKED_SCORE)
        row_max = diagonal.max(-1)
        level_terms = []
        for bit_level in range(levels):
            stride = 2 ** bit_level
            _, query_high = split_upper(query_part, 0, stride)
            key_low, _ = split_upper(key_part, 0, stride)
            value_low, _ = split_upper(value_part, 0, stride)
            _, bits_high = split_upper(head_bits, 0, stride)
            allowed = jnp.right_shift(bits_high, bit_level) & 1 == 1
            scores = jnp.einsum('nqd,nkd->nqk', query_high, key_low) * scaling
            scores = jnp.where(allowed[:, None, None], scores, MASKED_SCORE)
            upper_max = scores.max(-1)
            row_max = jnp.maximum(row_max, join_halves(jnp.full_like(upper_max, MASKED_SCORE), upper_max, 0, stride))
            level_terms.append((bit_level, scores, value_low))
        weights = jnp.exp(diagonal - row_max[..., None])
        row_sum = weights.sum(-1)
        result = jnp.einsum('nqk,nkd->nqd', round_weights(weights), value_part)
        for bit_level, scores, value_low in level_terms:
            stride = 2 ** bit_level
            _, max_high = split_upper(row_max, 0, stride)
            weights = jnp.exp(scores - max_high[..., None])
            sum_high = weights.sum(-1)
            result_high = jnp.einsum('nqk,nkd->nqd', round_weights(weights), value_low)
            row_sum = row_sum + join_halves(jnp.zeros_like(sum_high), sum_high, 0, stride)
            result = result + join_halves(jnp.zeros_like(result_high), result_high, 0, stride)
        return (result / row_sum[..., None]).astype(jnp.bfloat16)
    attended = lax.map(one_head, jnp.arange(QH, dtype=jnp.int32))
    attended = attended.transpose(1, 2, 0, 3).reshape(sequence, QH * DH)
    summed = residual.astype(jnp.float32) + attended.astype(jnp.float32)
    stream = summed.astype(jnp.bfloat16)
    normed = summed * lax.rsqrt(lax.optimization_barrier(jnp.mean(summed * summed, axis=-1, keepdims=True)) + EPSILON) * norm_gain.astype(jnp.float32)
    return (stream, normed.astype(jnp.bfloat16))
```

```python
import functools

import jax
import jax.numpy as jnp
from jax import lax
from jax.experimental import pallas as pl
from jax.experimental.pallas import tpu as pltpu
from jax.sharding import PartitionSpec as P

DH = 128
BLOCK = 128
EPSILON = 1e-05
NEG = -1e30
KERNEL_VMEM = 16 * 2**20
SCALE = DH ** (-0.5) * 1.4426950408889634
LATE = 2


def pairs(size, bit):
    return [(i - 2**bit, i) for i in range(size) if (i >> bit) & 1]


def params():
    return pltpu.CompilerParams(vmem_limit_bytes=KERNEL_VMEM)


def rows_at(index):
    return pl.ds(pl.multiple_of(index * BLOCK, BLOCK), BLOCK)


def column(tile, lane):
    return tile[:, lane : lane + 1]


def scores_of(q, k):
    return lax.dot_general(q, k, (((1,), (1,)), ((), ())), preferred_element_type=jnp.float32) * SCALE


def order_kernel(place_ref, k_ref, v_ref, all_ref, late_ref, rest_ref):
    blocks = k_ref.shape[0] // BLOCK
    for n in range(blocks):
        source = rows_at(place_ref[0] ^ n)
        key, val = k_ref[source, :], v_ref[source, :]
        part, at = (late_ref, n) if n < LATE else (rest_ref, n - LATE)
        for ref, first in ((all_ref, n), (part, at)):
            ref[first * BLOCK : (first + 1) * BLOCK, :DH] = key
            ref[first * BLOCK : (first + 1) * BLOCK, DH:] = val


def ordered(place, keys, values):
    rows = keys.shape[0]
    vmem = pl.BlockSpec(memory_space=pltpu.VMEM)
    return pl.pallas_call(
        order_kernel,
        in_specs=[pl.BlockSpec(memory_space=pltpu.SMEM), vmem, vmem],
        out_specs=[vmem] * 3,
        out_shape=[
            jax.ShapeDtypeStruct((n, 2 * DH), jnp.bfloat16)
            for n in (rows, LATE * BLOCK, rows - LATE * BLOCK)
        ],
        compiler_params=params(),
        name="order",
    )(place, keys, values)


def attend(q, keys, vals, biases, causal=None, before=None):
    s = scores_of(q, jnp.concatenate(keys, 0))
    parts = []
    for n, bias in enumerate(biases):
        part = s[:, n * BLOCK : (n + 1) * BLOCK]
        parts.append(jnp.where(causal, part, NEG) if bias is None else part + bias)
    top = functools.reduce(jnp.maximum, parts).max(-1, keepdims=True)
    if before is not None:
        top = jnp.maximum(top, before[1])
    weights = [jnp.exp2(part - top) for part in parts]
    total = functools.reduce(jnp.add, weights).sum(-1, keepdims=True)
    weight = jnp.concatenate([w.astype(jnp.bfloat16) for w in weights], 1)
    summed = jnp.dot(weight, jnp.concatenate(vals, 0), preferred_element_type=jnp.float32)
    if before is not None:
        factor = jnp.exp2(before[1] - top)
        total = total + factor
        summed = summed + before[0] * factor
    return summed / total, top + jnp.log2(total)


def bias_of(bitmap, level):
    allowed = lax.shift_right_logical(bitmap, level) & 1
    return (1 - allowed).astype(jnp.float32) * NEG


def local_kernel(heads, levels, place_ref, mask_ref, q_ref, kv_ref, part_ref, stat_ref):
    n = pl.program_id(0)
    j = place_ref[0] ^ n
    bits = [lax.shift_right_logical(j, b) & 1 for b in range(levels)]
    count = sum(bits)
    lanes = lax.broadcasted_iota(jnp.int32, (BLOCK, BLOCK), 1)
    causal = lax.broadcasted_iota(jnp.int32, (BLOCK, BLOCK), 0) >= lanes

    def body(number):
        chosen = []
        for at in range(number):
            level, seen = 0, 0
            for b, bit in enumerate(bits):
                level = level + jnp.where((bit == 1) & (seen == at), b, 0)
                seen = seen + bit
            chosen.append(level)
        blocks = [kv_ref[rows_at(n), :]]
        for level in chosen:
            blocks.append(kv_ref[rows_at(n ^ lax.shift_left(jnp.int32(1), level)), :])
        keys, vals = [b[:, :DH] for b in blocks], [b[:, DH:] for b in blocks]
        stats = jnp.zeros((BLOCK, BLOCK), jnp.float32)
        for h in range(heads):
            at = slice(h * DH, (h + 1) * DH)
            biases = [None] + [bias_of(mask_ref[h, j], level) for level in chosen]
            result, logsum = attend(q_ref[:, at], keys, vals, biases, causal)
            part_ref[0, :, at] = result
            stats = jnp.where(lanes == h, logsum, stats)
        stat_ref[0] = stats

    for number in range(levels + 1):
        pl.when(count == number)(functools.partial(body, number))


def local_part(place, block_masks, queries, kv):
    tokens, width = queries.shape
    heads, blocks = block_masks.shape
    return pl.pallas_call(
        functools.partial(local_kernel, heads, blocks.bit_length() - 1),
        grid_spec=pltpu.PrefetchScalarGridSpec(
            num_scalar_prefetch=2,
            grid=(blocks,),
            in_specs=[
                pl.BlockSpec((BLOCK, width), lambda n, place, mask: (place[0] ^ n, 0)),
                pl.BlockSpec(kv.shape, lambda n, place, mask: (0, 0)),
            ],
            out_specs=[
                pl.BlockSpec((1, BLOCK, width), lambda n, place, mask: (n, 0, 0)),
                pl.BlockSpec((1, BLOCK, BLOCK), lambda n, place, mask: (n, 0, 0)),
            ],
        ),
        out_shape=[
            jax.ShapeDtypeStruct((blocks, BLOCK, width), jnp.float32),
            jax.ShapeDtypeStruct((blocks, BLOCK, BLOCK), jnp.float32),
        ],
        cost_estimate=pl.CostEstimate(
            flops=3 * 4 * tokens * width * BLOCK, bytes_accessed=4_000_000, transcendentals=3 * tokens * heads * BLOCK
        ),
        compiler_params=params(),
        name="local",
    )(place, block_masks, queries, kv)


def far_kernel(heads, levels, first, final, place_ref, mask_ref, q_ref, part_ref, stat_ref, *refs):
    kv_refs, outs = refs[: len(levels)], refs[len(levels) :]
    i = pl.program_id(0)
    j = place_ref[0] ^ (i + first)
    lanes = lax.broadcasted_iota(jnp.int32, (BLOCK, BLOCK), 1)
    keys = [ref[:, :DH] for ref in kv_refs]
    vals = [ref[:, DH:] for ref in kv_refs]
    stats = stat_ref[0]
    new = jnp.zeros((BLOCK, BLOCK), jnp.float32)
    results = []
    for h in range(heads):
        at = slice(h * DH, (h + 1) * DH)
        bitmap = mask_ref[h, j] & place_ref[1]
        biases = [bias_of(bitmap, level) for level in levels]
        result, logsum = attend(q_ref[:, at], keys, vals, biases, None, (part_ref[0, :, at], column(stats, h)))
        if final:
            results.append(result.astype(jnp.bfloat16))
        else:
            outs[0][0, :, at] = result
            new = jnp.where(lanes == h, logsum, new)
    if final:
        whole = jnp.concatenate(results, 1)
        for n, out in enumerate(outs):

            @pl.when(i == n)
            def _(out=out):
                out[...] = whole
    else:
        outs[1][0] = new


def far_part(place, block_masks, queries, part, stats, kvs, levels, first, count, final):
    tokens, width = queries.shape
    heads, blocks = block_masks.shape

    def blocked(array):
        held = array.shape[0]
        offset = first if held == blocks else 0
        return pl.BlockSpec((1,) + array.shape[1:], lambda i, place, mask: (i + offset, 0, 0))

    def keyed(array):
        offset = first if array.shape[0] == tokens else 0
        return pl.BlockSpec((BLOCK, 2 * DH), lambda i, place, mask: (i + offset, 0))

    if final:
        out_specs = [pl.BlockSpec((BLOCK, width), lambda i, place, mask: (0, 0))] * count
        out_shape = [jax.ShapeDtypeStruct((BLOCK, width), jnp.bfloat16)] * count
    else:
        out_specs = [
            pl.BlockSpec((1, BLOCK, width), lambda i, place, mask: (i, 0, 0)),
            pl.BlockSpec((1, BLOCK, BLOCK), lambda i, place, mask: (i, 0, 0)),
        ]
        out_shape = [
            jax.ShapeDtypeStruct((count, BLOCK, width), jnp.float32),
            jax.ShapeDtypeStruct((count, BLOCK, BLOCK), jnp.float32),
        ]
    return pl.pallas_call(
        functools.partial(far_kernel, heads, levels, first, final),
        grid_spec=pltpu.PrefetchScalarGridSpec(
            num_scalar_prefetch=2,
            grid=(count,),
            in_specs=[
                pl.BlockSpec((BLOCK, width), lambda i, place, mask: (place[0] ^ (i + first), 0)),
                blocked(part),
                blocked(stats),
            ]
            + [keyed(kv) for kv in kvs],
            out_specs=out_specs,
        ),
        out_shape=out_shape,
        cost_estimate=pl.CostEstimate(
            flops=len(kvs) * 4 * count * BLOCK * width * BLOCK,
            bytes_accessed=4_000_000,
            transcendentals=len(kvs) * count * heads * BLOCK * BLOCK,
        ),
        compiler_params=params(),
        name="far",
    )(place, block_masks, queries, part, stats, *kvs)


def norm_kernel(groups, place_ref, *refs):
    parts = refs[:groups]
    res_ref, gain_ref, stream_ref, normed_ref, whole = refs[groups:]
    width = parts[0].shape[1]
    square = jnp.zeros((BLOCK, DH), jnp.float32)
    for n in range(groups):
        cols = pl.ds(pl.multiple_of((place_ref[0] ^ n) * width, width), width)
        summed = res_ref[:, cols].astype(jnp.float32) + parts[n][...].astype(jnp.float32)
        stream_ref[:, cols] = summed.astype(jnp.bfloat16)
        whole[:, cols] = summed
        for c in range(0, width, DH):
            piece = summed[:, c : c + DH]
            square = square + piece * piece
    mean = square.sum(-1, keepdims=True) / (groups * width)
    factor = lax.rsqrt(mean + EPSILON)
    for n in range(groups):
        cols = slice(n * width, (n + 1) * width)
        normed_ref[:, cols] = (whole[:, cols] * factor * gain_ref[:, cols].astype(jnp.float32)).astype(jnp.bfloat16)


def norm_part(place, parts, residual, gain):
    vmem = pl.BlockSpec(memory_space=pltpu.VMEM)
    return pl.pallas_call(
        functools.partial(norm_kernel, len(parts)),
        in_specs=[pl.BlockSpec(memory_space=pltpu.SMEM)] + [vmem] * (len(parts) + 2),
        out_specs=[vmem] * 2,
        out_shape=[jax.ShapeDtypeStruct(residual.shape, jnp.bfloat16)] * 2,
        scratch_shapes=[pltpu.VMEM(residual.shape, jnp.float32)],
        cost_estimate=pl.CostEstimate(flops=4_000_000, bytes_accessed=4_000_000, transcendentals=128),
        compiler_params=params(),
        name="norm",
    )(place, *parts, residual, gain)


def shards(queries, keys, values, block_masks, residual, norm_gain):
    _, blocks = block_masks.shape
    ctx_size = lax.axis_size("ctx")
    groups = lax.axis_size("head")
    local_bits = blocks.bit_length() - 1
    place = jnp.stack([lax.axis_index("head"), lax.axis_index("ctx") * blocks]).astype(jnp.int32)

    def fetched(array, bit):
        return lax.ppermute(array, "ctx", pairs(ctx_size, bit))

    def swapped(array, n):
        return lax.ppermute(array, "head", [(i, i ^ n) for i in range(groups)])

    def level(bits):
        return [local_bits + b for b in bits]

    kv, kv_late, kv_rest = ordered(place, keys, values)
    rest = {b: fetched(kv_rest, b) for b in (2, 1, 0)}
    far = {b: fetched(kv, b) for b in (4, 3)}
    late = {b: fetched(kv_late, b) for b in (2, 1, 0)}
    part, stats = local_part(place, block_masks, queries, kv)
    part, stats = far_part(place, block_masks, queries, part, stats, [far[4], far[3]], level((4, 3)), 0, blocks, False)
    sent = far_part(
        place,
        block_masks,
        queries,
        part,
        stats,
        [rest[b] for b in (2, 1, 0)],
        level((2, 1, 0)),
        LATE,
        blocks - LATE,
        True,
    )
    kept = far_part(
        place,
        block_masks,
        queries,
        part,
        stats,
        [late[b] for b in (2, 1, 0)],
        level((2, 1, 0)),
        0,
        LATE,
        True,
    )
    parts = [kept[0]] + [swapped(kept[n], n) for n in range(1, LATE)]
    parts += [swapped(sent[n - LATE], n) for n in range(LATE, blocks)]
    return norm_part(place, parts, residual, norm_gain.reshape(1, -1))


def solution(mesh):
    in_specs = (
        P("ctx", "head"),
        P("ctx", "head"),
        P("ctx", "head"),
        P("head", "ctx"),
        P(("ctx", "head"), None),
        P(),
    )
    out_specs = (P(("ctx", "head"), None), P(("ctx", "head"), None))
    return jax.shard_map(shards, mesh=mesh, in_specs=in_specs, out_specs=out_specs, check_vma=False)
```

```python
import functools

import jax
import jax.numpy as jnp
from jax import lax
from jax.experimental import pallas as pl
from jax.experimental.pallas import tpu as pltpu
from jax.sharding import PartitionSpec as P

DH = 128
BLOCK = 128
EPSILON = 1e-05
NEG = -1e30
KERNEL_VMEM = 16 * 2**20
SCALE = DH ** (-0.5) * 1.4426950408889634
LATE = 3


NEAR, SIDE, HALF, FOURTH, THIRD = 1, 2, 3, 4, 5


def slots(size):
    pairs = {slot: [] for slot in (NEAR, SIDE, HALF, FOURTH, THIRD)}
    for i in range(size):
        low = i & 3
        for slot, bit, taken in (
            (NEAR, 0, low == 3),
            (NEAR, 1, low == 2),
            (SIDE, 0, low == 1),
            (SIDE, 1, low == 3),
            (HALF, 2, i & 4),
            (THIRD, 3, i & 8),
            (FOURTH, 4, i & 16),
        ):
            if taken:
                pairs[slot].append((i - 2**bit, i))
    return pairs


def slot_level(slot, ctx, local_bits):
    bit = [lax.shift_right_logical(ctx, b) & 1 for b in range(5)]
    taken, level = {
        NEAR: (bit[1], 1 - bit[0]),
        SIDE: (bit[0], bit[1]),
        HALF: (bit[2], 2),
        FOURTH: (bit[4], 4),
        THIRD: (bit[3], 3),
    }[slot]
    return jnp.where(taken == 1, local_bits + level, 31)


def held_in(space, *arrays):
    return [pltpu.with_memory_space_constraint(array, space) for array in arrays]


def params():
    return pltpu.CompilerParams(vmem_limit_bytes=KERNEL_VMEM)


def rows_at(index):
    return pl.ds(pl.multiple_of(index * BLOCK, BLOCK), BLOCK)


def in_vmem():
    return pl.BlockSpec(memory_space=pltpu.VMEM)


def order_kernel(place_ref, k_hbm, v_hbm, all_ref, late_ref, rest_ref, k_ref, v_ref, sems):
    copies = [pltpu.make_async_copy(k_hbm, k_ref, sems.at[0]), pltpu.make_async_copy(v_hbm, v_ref, sems.at[1])]
    for copy in copies:
        copy.start()
    for copy in copies:
        copy.wait()
    blocks = k_ref.shape[0] // BLOCK
    for n in range(blocks):
        source = rows_at(place_ref[0] ^ n)
        key, val = k_ref[source, :], v_ref[source, :].T
        part, at = (late_ref, n) if n < LATE else (rest_ref, n - LATE)
        for ref, first in ((all_ref, n), (part, at)):
            ref[first * BLOCK : (first + 1) * BLOCK, :DH] = key
            ref[first * BLOCK : (first + 1) * BLOCK, DH:] = val


def ordered(place, keys, values):
    rows = keys.shape[0]
    hbm = pl.BlockSpec(memory_space=pl.ANY)
    return pl.pallas_call(
        order_kernel,
        in_specs=[pl.BlockSpec(memory_space=pltpu.SMEM), hbm, hbm],
        out_specs=[in_vmem()] * 3,
        out_shape=[
            jax.ShapeDtypeStruct((n, 2 * DH), jnp.bfloat16)
            for n in (rows, LATE * BLOCK, rows - LATE * BLOCK)
        ],
        scratch_shapes=[pltpu.VMEM(keys.shape, jnp.bfloat16)] * 2 + [pltpu.SemaphoreType.DMA((2,))],
        compiler_params=params(),
        name="order",
    )(place, *held_in(pltpu.HBM, keys, values))


def attend(q, keys, vals, biases, causal=None, before=None):
    scores = lax.dot_general(
        jnp.concatenate(keys, 0), q, (((1,), (1,)), ((), ())), preferred_element_type=jnp.float32
    )
    parts = [scores[n * BLOCK : (n + 1) * BLOCK, :] for n in range(len(keys))]
    if causal is not None:
        parts[0] = jnp.where(causal, parts[0], NEG)
    tops = [part.max(0, keepdims=True) * SCALE + bias for part, bias in zip(parts, biases)]
    top = functools.reduce(jnp.maximum, tops if before is None else [before[1]] + tops)
    weights = [jnp.exp2(part * SCALE - (top - bias)) for part, bias in zip(parts, biases)]
    total = functools.reduce(jnp.add, weights).sum(0, keepdims=True)
    weight = jnp.concatenate([w.astype(jnp.bfloat16) for w in weights], 0)
    summed = jnp.dot(jnp.concatenate(vals, 1), weight, preferred_element_type=jnp.float32)
    if before is not None:
        factor = jnp.exp2(before[1] - top)
        total = total + before[2] * factor
        summed = summed + before[0] * factor
    return summed, top, total


def bias_of(bitmaps, level):
    pieces = []
    for bitmap in bitmaps:
        allowed = lax.shift_right_logical(bitmap, level) & 1
        pieces.append(jnp.full((1, BLOCK), (1 - allowed).astype(jnp.float32) * NEG))
    return jnp.concatenate(pieces, 1)


def local_kernel(heads, blocks, place_ref, mask_ref, q_hbm, kv_ref, q_ref, part_ref, stat_ref, sems):
    rank = place_ref[0]
    copies = []
    for j in range(blocks):
        for h in range(heads):
            copies.append(
                pltpu.make_async_copy(
                    q_hbm.at[j * BLOCK : (j + 1) * BLOCK, h * DH : (h + 1) * DH],
                    q_ref.at[rank ^ j, h * BLOCK : (h + 1) * BLOCK, :],
                    sems.at[j, h],
                )
            )
    for copy in copies:
        copy.start()
    shape = (BLOCK, heads * BLOCK)
    causal = lax.broadcasted_iota(jnp.int32, shape, 0) <= (lax.broadcasted_iota(jnp.int32, shape, 1) & (BLOCK - 1))
    for copy in copies:
        copy.wait()
    for j in range(blocks):
        levels = [b for b in range(blocks.bit_length() - 1) if j >> b & 1]
        held = [kv_ref[rows_at(rank ^ other), :] for other in [j] + [j - 2**b for b in levels]]
        bitmaps = [mask_ref[h, j] for h in range(heads)]
        biases = [0.0] + [bias_of(bitmaps, level) for level in levels]
        summed, top, total = attend(
            q_ref[rank ^ j], [kv[:, :DH] for kv in held], [kv[:, DH:] for kv in held], biases, causal
        )
        part_ref[rank ^ j] = summed
        stat_ref[rank ^ j, 0:1, :] = top
        stat_ref[rank ^ j, 1:2, :] = total


def local_part(place, block_masks, queries, kv):
    tokens, width = queries.shape
    heads, blocks = block_masks.shape
    smem = pl.BlockSpec(memory_space=pltpu.SMEM)
    return pl.pallas_call(
        functools.partial(local_kernel, heads, blocks),
        in_specs=[smem, smem, pl.BlockSpec(memory_space=pl.ANY), in_vmem()],
        out_specs=[in_vmem()] * 3,
        out_shape=[
            jax.ShapeDtypeStruct((blocks, heads * BLOCK, DH), jnp.bfloat16),
            jax.ShapeDtypeStruct((blocks, DH, width), jnp.float32),
            jax.ShapeDtypeStruct((blocks, 8, width), jnp.float32),
        ],
        scratch_shapes=[pltpu.SemaphoreType.DMA((blocks, heads))],
        cost_estimate=pl.CostEstimate(
            flops=3 * 4 * tokens * width * BLOCK, bytes_accessed=4_000_000, transcendentals=3 * tokens * heads * BLOCK
        ),
        compiler_params=params(),
        name="local",
    )(place, block_masks, *held_in(pltpu.HBM, queries), kv)


def far_kernel(heads, local_bits, held, first, count, offset, final, place_ref, mask_ref, q_ref, part_ref, stat_ref, *refs):
    arrays = sum(number for _, number in held)
    kv_refs, outs = refs[:arrays], refs[arrays:]
    levels = [slot_level(slot, place_ref[1], local_bits) for slot, _ in held]
    for i in range(count):
        n = first + i
        j = place_ref[0] ^ n
        keys, vals, rest = [], [], kv_refs
        for _, number in held:
            tiles = []
            for ref in rest[:number]:
                at = (n if ref.shape[0] == q_ref.shape[0] * BLOCK else i) * BLOCK
                tiles.append(ref[at : at + BLOCK, :])
            rest = rest[number:]
            tile = functools.reduce(jnp.add, tiles)
            keys.append(tile[:, :DH])
            vals.append(tile[:, DH:])
        bitmaps = [mask_ref[h, j] for h in range(heads)]
        biases = [bias_of(bitmaps, level) for level in levels]
        before = (part_ref[offset + i], stat_ref[offset + i, 0:1, :], stat_ref[offset + i, 1:2, :])
        summed, top, total = attend(q_ref[n], keys, vals, biases, None, before)
        if final:
            result = summed * (1.0 / total)
            for h in range(heads):
                at = slice(h * DH, (h + 1) * DH)
                tile = result[:, at].T.astype(jnp.bfloat16)
                if final == "ranks":
                    outs[0][rows_at(j), at] = tile
                else:
                    outs[i][:, at] = tile
        else:
            outs[0][i] = summed
            outs[1][i, 0:1, :] = top
            outs[1][i, 1:2, :] = total


def far_part(place, block_masks, state, fetched, held, first, count, final=None):
    queries, part, stats = state
    heads, blocks = block_masks.shape
    width = heads * DH
    kvs = []
    numbers = []
    for slot in held:
        arrays = fetched[slot] if isinstance(fetched[slot], list) else [fetched[slot]]
        kvs += arrays
        numbers.append((slot, len(arrays)))
    if final == "ranks":
        out_shape = [jax.ShapeDtypeStruct((blocks * BLOCK, width), jnp.bfloat16)]
    elif final == "order":
        out_shape = [jax.ShapeDtypeStruct((BLOCK, width), jnp.bfloat16)] * count
    else:
        out_shape = [
            jax.ShapeDtypeStruct((count, DH, width), jnp.float32),
            jax.ShapeDtypeStruct((count, 8, width), jnp.float32),
        ]
    smem = pl.BlockSpec(memory_space=pltpu.SMEM)
    offset = first if part.shape[0] == blocks else 0
    outs = pl.pallas_call(
        functools.partial(far_kernel, heads, blocks.bit_length() - 1, numbers, first, count, offset, final),
        in_specs=[smem, smem] + [in_vmem()] * (3 + len(kvs)),
        out_specs=[in_vmem()] * len(out_shape),
        out_shape=out_shape,
        cost_estimate=pl.CostEstimate(
            flops=len(kvs) * 4 * count * BLOCK * width * BLOCK,
            bytes_accessed=4_000_000,
            transcendentals=len(kvs) * count * heads * BLOCK * BLOCK,
        ),
        compiler_params=params(),
        name="far",
    )(place, block_masks, queries, part, stats, *kvs)
    if final:
        return outs
    return [queries] + list(outs)


def norm_kernel(groups, place_ref, *refs):
    near, (far_ref, res_ref, gain_ref, stream_ref, normed_ref, whole) = refs[:LATE], refs[LATE:]
    width = near[0].shape[1]
    square = jnp.zeros((BLOCK, DH), jnp.float32)
    for n in range(groups):
        source = place_ref[0] ^ n
        cols = pl.ds(pl.multiple_of(source * width, width), width)
        attended = near[n][...] if n < LATE else far_ref[rows_at(source), :]
        summed = res_ref[:, cols].astype(jnp.float32) + attended.astype(jnp.float32)
        stream_ref[:, cols] = summed.astype(jnp.bfloat16)
        whole[:, cols] = summed
        for c in range(0, width, DH):
            piece = summed[:, c : c + DH]
            square = square + piece * piece
    mean = square.sum(-1, keepdims=True) / (groups * width)
    factor = lax.rsqrt(mean + EPSILON)
    for n in range(groups):
        cols = slice(n * width, (n + 1) * width)
        normed_ref[:, cols] = (whole[:, cols] * factor * gain_ref[:, cols].astype(jnp.float32)).astype(jnp.bfloat16)


def norm_part(place, near, far, residual, gain):
    vmem = pl.BlockSpec(memory_space=pltpu.VMEM)
    return pl.pallas_call(
        functools.partial(norm_kernel, far.shape[0] // BLOCK),
        in_specs=[pl.BlockSpec(memory_space=pltpu.SMEM)] + [vmem] * (len(near) + 3),
        out_specs=[vmem] * 2,
        out_shape=[jax.ShapeDtypeStruct(residual.shape, jnp.bfloat16)] * 2,
        scratch_shapes=[pltpu.VMEM(residual.shape, jnp.float32)],
        cost_estimate=pl.CostEstimate(flops=4_000_000, bytes_accessed=4_000_000, transcendentals=128),
        compiler_params=params(),
        name="norm",
    )(place, *near, far, residual, gain)


def shards(queries, keys, values, block_masks, residual, norm_gain):
    _, blocks = block_masks.shape
    groups = lax.axis_size("head")
    routes = slots(lax.axis_size("ctx"))
    place = jnp.stack([lax.axis_index("head"), lax.axis_index("ctx")]).astype(jnp.int32)

    def fetched(array, slot):
        return lax.ppermute(array, "ctx", routes[slot])

    def swapped(array, n):
        return lax.ppermute(array, "head", [(i, i ^ n) for i in range(groups)])

    by_three = [(i - 3, i) for i in range(lax.axis_size("ctx")) if i & 7 == 6]

    kv, kv_late, kv_rest = ordered(place, keys, values)
    far = {slot: fetched(kv, slot) for slot in (FOURTH, THIRD)}
    rest = far | {slot: fetched(kv_rest, slot) for slot in (NEAR, SIDE)}
    straight = [(i, j) for i, j in routes[HALF] if j & 7 != 6]
    rest[HALF] = [lax.ppermute(kv_rest, "ctx", straight)]
    rest[HALF] += [lax.ppermute(rest[NEAR], "ctx", by_three)]
    late = far | {slot: fetched(kv_late, slot) for slot in (NEAR, SIDE, HALF)}
    given = (place, block_masks)
    state = local_part(place, block_masks, queries, kv)
    rest_state = far_part(*given, state, rest, (NEAR, SIDE, FOURTH, THIRD), LATE, blocks - LATE)
    (sent,) = far_part(*given, rest_state, rest, (HALF,), LATE, blocks - LATE, "ranks")
    received = lax.all_to_all(sent, "head", split_axis=0, concat_axis=0, tiled=True)
    late_state = far_part(*given, state, late, (FOURTH, THIRD), 0, LATE)
    near = far_part(*given, late_state, late, (NEAR, SIDE, HALF), 0, LATE, "order")
    near = [near[0]] + [swapped(near[n], n) for n in range(1, LATE)]
    return norm_part(place, near, received, residual, norm_gain.reshape(1, -1))


def solution(mesh):
    in_specs = (
        P("ctx", "head"),
        P("ctx", "head"),
        P("ctx", "head"),
        P("head", "ctx"),
        P(("ctx", "head"), None),
        P(),
    )
    out_specs = (P(("ctx", "head"), None), P(("ctx", "head"), None))
    return jax.shard_map(shards, mesh=mesh, in_specs=in_specs, out_specs=out_specs, check_vma=False)
```

```python
import functools

import jax
import jax.numpy as jnp
from jax import lax
from jax.experimental import pallas as pl
from jax.experimental.pallas import tpu as pltpu
from jax.sharding import PartitionSpec as P

DH = 128
BLOCK = 128
BLOCKS = 8
HEADS = 4
EPSILON = 1e-05
NEG = -1e30
KERNEL_VMEM = 16 * 2**20
SCALE = DH ** (-0.5) * 1.4426950408889634
LATE = 2
FIRST = 2
SWAPS = [n for n in (6, 4, 7, 5, 3, 2) if n >= LATE]


NEAR, SIDE, HALF, FOURTH, THIRD = 1, 2, 3, 4, 5
SIDE_ONWARD, HALF_STRAIGHT = 6, 7


def slots(size):
    pairs = {slot: [] for slot in (NEAR, SIDE, HALF, FOURTH, THIRD)}
    for i in range(size):
        low = i & 3
        for slot, bit, taken in (
            (NEAR, 0, low == 3),
            (NEAR, 1, low == 2),
            (SIDE, 0, low == 1),
            (SIDE, 1, low == 3),
            (HALF, 2, i & 4),
            (THIRD, 3, i & 8),
            (FOURTH, 4, i & 16),
        ):
            if taken:
                pairs[slot].append((i - 2**bit, i))
    return pairs


def slot_level(slot, ctx, local_bits):
    bit = [lax.shift_right_logical(ctx, b) & 1 for b in range(5)]
    six = bit[2] & bit[1] & (1 - bit[0])
    taken, level = {
        SIDE_ONWARD: (bit[0] | six, jnp.where(six == 1, 2, bit[1])),
        HALF_STRAIGHT: (bit[2] & (1 - six), 2),
        NEAR: (bit[1], 1 - bit[0]),
        SIDE: (bit[0], bit[1]),
        HALF: (bit[2], 2),
        FOURTH: (bit[4], 4),
        THIRD: (bit[3], 3),
    }[slot]
    return jnp.where(taken == 1, local_bits + level, 31)


def held_in(space, *arrays):
    return [pltpu.with_memory_space_constraint(array, space) for array in arrays]


def params():
    return pltpu.CompilerParams(vmem_limit_bytes=KERNEL_VMEM)


def rows_at(index):
    return pl.ds(pl.multiple_of(index * BLOCK, BLOCK), BLOCK)


def in_vmem():
    return pl.BlockSpec(memory_space=pltpu.VMEM)


def order_kernel(info_ref, k_hbm, v_hbm, q_hbm, all_ref, late_ref, rest_ref, q_ref, k_ref, v_ref, sems):
    rank = info_ref[0, 0]
    copies = [pltpu.make_async_copy(k_hbm, k_ref, sems.at[0, 0]), pltpu.make_async_copy(v_hbm, v_ref, sems.at[0, 1])]
    for n in range(BLOCKS):
        for h in range(HEADS):
            source = q_hbm.at[rows_at(rank ^ n), h * DH : (h + 1) * DH]
            copies.append(
                pltpu.make_async_copy(source, q_ref.at[n, h * BLOCK : (h + 1) * BLOCK, :], sems.at[1 + n, h])
            )
    for copy in copies:
        copy.start()
    for copy in copies[:2]:
        copy.wait()
    for n in range(BLOCKS):
        source = rows_at(rank ^ n)
        key, val = k_ref[source, :], v_ref[source, :].T
        part, at = (late_ref, n) if n < LATE else (rest_ref, n - LATE)
        for ref, first in ((all_ref, n), (part, at)):
            ref[first * BLOCK : (first + 1) * BLOCK, :DH] = key
            ref[first * BLOCK : (first + 1) * BLOCK, DH:] = val
    for copy in copies[2:]:
        copy.wait()


def ordered(info, keys, values, queries):
    rows = keys.shape[0]
    hbm = pl.BlockSpec(memory_space=pl.ANY)
    return pl.pallas_call(
        order_kernel,
        in_specs=[pl.BlockSpec(memory_space=pltpu.SMEM), hbm, hbm, hbm],
        out_specs=[in_vmem()] * 4,
        out_shape=[
            jax.ShapeDtypeStruct((n, 2 * DH), jnp.bfloat16)
            for n in (rows, LATE * BLOCK, rows - LATE * BLOCK)
        ]
        + [jax.ShapeDtypeStruct((BLOCKS, HEADS * BLOCK, DH), jnp.bfloat16)],
        scratch_shapes=[pltpu.VMEM(keys.shape, jnp.bfloat16)] * 2 + [pltpu.SemaphoreType.DMA((1 + BLOCKS, HEADS))],
        compiler_params=params(),
        name="order",
    )(info, *held_in(pltpu.HBM, keys, values, queries))


def attend(q, keys, vals, biases, causal=None, before=None):
    scores = lax.dot_general(
        jnp.concatenate(keys, 0), q, (((1,), (1,)), ((), ())), preferred_element_type=jnp.float32
    )
    parts = [scores[n * BLOCK : (n + 1) * BLOCK, :] for n in range(len(keys))]
    if causal is not None:
        parts[0] = jnp.where(causal, parts[0], NEG)
    tops = [part.max(0, keepdims=True) * SCALE + bias for part, bias in zip(parts, biases)]
    top = functools.reduce(jnp.maximum, tops if before is None else [before[1]] + tops)
    weights = [jnp.exp2(part * SCALE - (top - bias)) for part, bias in zip(parts, biases)]
    total = functools.reduce(jnp.add, weights).sum(0, keepdims=True)
    weight = jnp.concatenate([w.astype(jnp.bfloat16) for w in weights], 0)
    summed = jnp.dot(jnp.concatenate(vals, 1), weight, preferred_element_type=jnp.float32)
    if before is not None:
        factor = jnp.exp2(before[1] - top)
        total = total + before[2] * factor
        summed = summed + before[0] * factor
    return summed, top, total


def bitmap_at(info_ref, h, j):
    return info_ref[1 + h, j]


def bias_of(bitmaps, level):
    pieces = []
    for bitmap in bitmaps:
        allowed = lax.shift_right_logical(bitmap, level) & 1
        pieces.append(jnp.full((1, BLOCK), (1 - allowed).astype(jnp.float32) * NEG))
    return jnp.concatenate(pieces, 1)


def local_kernel(first, count, turn, info_ref, q_ref, kv_ref, *refs):
    part_ref, stat_ref = refs[-2:]
    rank = info_ref[0, 0]

    def body():
        shape = (BLOCK, HEADS * BLOCK)
        causal = lax.broadcasted_iota(jnp.int32, shape, 0) <= (
            lax.broadcasted_iota(jnp.int32, shape, 1) & (BLOCK - 1)
        )
        for i in range(count):
            n = first + i
            j = rank ^ n
            levels = range(BLOCKS.bit_length() - 1)
            others = [n] + [n ^ 2**b for b in levels]
            held = [kv_ref[m * BLOCK : (m + 1) * BLOCK, :] for m in others]
            bitmaps = [bitmap_at(info_ref, h, j) & j for h in range(HEADS)]
            biases = [0.0] + [bias_of(bitmaps, level) for level in levels]
            summed, top, total = attend(
                q_ref[n], [kv[:, :DH] for kv in held], [kv[:, DH:] for kv in held], biases, causal
            )
            part_ref[i] = summed
            stat_ref[i, 0:1, :] = top
            stat_ref[i, 1:2, :] = total

    if turn is None:
        body()
    else:
        pl.when(((info_ref[0, 1] & 7) < FIRST) == (turn == 0))(body)


def local_part(info, queries, kv, first, count, turn=None, state=()):
    width = HEADS * DH
    return pl.pallas_call(
        functools.partial(local_kernel, first, count, turn),
        in_specs=[pl.BlockSpec(memory_space=pltpu.SMEM)] + [in_vmem()] * (2 + len(state)),
        out_specs=[in_vmem()] * 2,
        out_shape=[
            jax.ShapeDtypeStruct((count, DH, width), jnp.float32),
            jax.ShapeDtypeStruct((count, 8, width), jnp.float32),
        ],
        input_output_aliases={3 + n: n for n in range(len(state))},
        cost_estimate=pl.CostEstimate(
            flops=4 * 4 * count * BLOCK * width * BLOCK, bytes_accessed=4_000_000, transcendentals=4 * count * BLOCK * width
        ),
        compiler_params=params(),
        name="local",
    )(info, queries, kv, *state)


def far_kernel(held, first, count, final, info_ref, q_ref, part_ref, stat_ref, *refs):
    arrays = sum(number for _, number in held)
    kv_refs, outs = refs[:arrays], refs[arrays:]
    levels = [slot_level(slot, info_ref[0, 1], BLOCKS.bit_length() - 1) for slot, _ in held]
    blocks = [n - first for n in final] if final else range(count)
    for place, i in enumerate(blocks):
        j = info_ref[0, 0] ^ (first + i)
        keys, vals, rest = [], [], kv_refs
        for _, number in held:
            tiles = []
            for ref in rest[:number]:
                at = (first + i if ref.shape[0] == BLOCKS * BLOCK else i) * BLOCK
                tiles.append(ref[at : at + BLOCK, :])
            rest = rest[number:]
            tile = functools.reduce(jnp.add, tiles)
            keys.append(tile[:, :DH])
            vals.append(tile[:, DH:])
        bitmaps = [bitmap_at(info_ref, h, j) for h in range(HEADS)]
        biases = [bias_of(bitmaps, level) for level in levels]
        before = (part_ref[i], stat_ref[i, 0:1, :], stat_ref[i, 1:2, :])
        summed, top, total = attend(q_ref[first + i], keys, vals, biases, None, before)
        if final:
            result = summed * (1.0 / total)
            for h in range(HEADS):
                at = slice(h * DH, (h + 1) * DH)
                outs[place][:, at] = result[:, at].T.astype(jnp.bfloat16)
        else:
            outs[0][i] = summed
            outs[1][i, 0:1, :] = top
            outs[1][i, 1:2, :] = total


def far_part(info, queries, state, fetched, held, first, final=()):
    part, stats = state
    count, _, width = part.shape
    kvs, numbers = [], []
    for slot in held:
        arrays = fetched[slot] if isinstance(fetched[slot], list) else [fetched[slot]]
        kvs += arrays
        numbers.append((slot, len(arrays)))
    if final:
        out_shape = [jax.ShapeDtypeStruct((BLOCK, width), jnp.bfloat16)] * len(final)
    else:
        out_shape = [
            jax.ShapeDtypeStruct((count, DH, width), jnp.float32),
            jax.ShapeDtypeStruct((count, 8, width), jnp.float32),
        ]
    outs = pl.pallas_call(
        functools.partial(far_kernel, numbers, first, count, final),
        in_specs=[pl.BlockSpec(memory_space=pltpu.SMEM)] + [in_vmem()] * (3 + len(kvs)),
        out_specs=[in_vmem()] * len(out_shape),
        out_shape=out_shape,
        cost_estimate=pl.CostEstimate(
            flops=len(kvs) * 4 * count * BLOCK * width * BLOCK,
            bytes_accessed=4_000_000,
            transcendentals=len(kvs) * count * BLOCK * width,
        ),
        compiler_params=params(),
        name="far",
    )(info, *held_in(pltpu.VMEM, queries, part, stats, *kvs))
    return list(outs)


def norm_kernel(info_ref, *refs):
    parts = refs[:BLOCKS]
    res_ref, gain_ref, stream_hbm, normed_hbm, whole, stream_ref, normed_ref, sems = refs[BLOCKS:]
    width = parts[0].shape[1]
    square = jnp.zeros((BLOCK, DH), jnp.float32)
    copies = []
    for n in range(BLOCKS):
        source = info_ref[0, 0] ^ n
        cols = pl.ds(pl.multiple_of(source * width, width), width)
        summed = res_ref[:, cols].astype(jnp.float32) + parts[n][...].astype(jnp.float32)
        stream_ref[n] = summed.astype(jnp.bfloat16)
        copies.append(pltpu.make_async_copy(stream_ref.at[n], stream_hbm.at[:, cols], sems.at[0, n]))
        copies[-1].start()
        whole[n] = summed
        for c in range(0, width, DH):
            piece = summed[:, c : c + DH]
            square = square + piece * piece
    mean = square.sum(-1, keepdims=True) / (BLOCKS * width)
    factor = lax.rsqrt(mean + EPSILON)
    for n in range(BLOCKS):
        source = info_ref[0, 0] ^ n
        cols = pl.ds(pl.multiple_of(source * width, width), width)
        normed_ref[n] = (whole[n] * factor * gain_ref[:, cols].astype(jnp.float32)).astype(jnp.bfloat16)
        copies.append(pltpu.make_async_copy(normed_ref.at[n], normed_hbm.at[:, cols], sems.at[1, n]))
        copies[-1].start()
    for copy in copies:
        copy.wait()


def norm_part(info, parts, residual, gain):
    width = parts[0].shape[1]
    return pl.pallas_call(
        norm_kernel,
        in_specs=[pl.BlockSpec(memory_space=pltpu.SMEM)] + [in_vmem()] * (len(parts) + 2),
        out_specs=[pl.BlockSpec(memory_space=pl.ANY)] * 2,
        out_shape=[jax.ShapeDtypeStruct(residual.shape, jnp.bfloat16)] * 2,
        scratch_shapes=[
            pltpu.VMEM((BLOCKS, BLOCK, width), jnp.float32),
            pltpu.VMEM((BLOCKS, BLOCK, width), jnp.bfloat16),
            pltpu.VMEM((BLOCKS, BLOCK, width), jnp.bfloat16),
            pltpu.SemaphoreType.DMA((2, BLOCKS)),
        ],
        cost_estimate=pl.CostEstimate(flops=4_000_000, bytes_accessed=4_000_000, transcendentals=128),
        compiler_params=params(),
        name="norm",
    )(info, *held_in(pltpu.VMEM, *parts), residual, gain)


def shards(queries, keys, values, block_masks, residual, norm_gain):
    groups = lax.axis_size("head")
    routes = slots(lax.axis_size("ctx"))
    at = lax.broadcasted_iota(jnp.int32, (1, BLOCKS), 1)
    place = jnp.where(at == 0, lax.axis_index("head"), lax.axis_index("ctx")).astype(jnp.int32)
    info = jnp.concatenate([place, block_masks], 0)

    def fetched(array, slot):
        return lax.ppermute(array, "ctx", routes[slot])

    def swapped(array, n):
        return lax.ppermute(array, "head", [(i, i ^ n) for i in range(groups)])

    by_three = [(i - 3, i) for i in range(lax.axis_size("ctx")) if i & 7 == 6]

    kv, kv_late, kv_rest, queries = ordered(info, keys, values, queries)
    far = {slot: fetched(kv, slot) for slot in (FOURTH, THIRD)}
    rest = far | {slot: fetched(kv_rest, slot) for slot in (NEAR, SIDE)}
    straight = [(i, j) for i, j in routes[HALF] if j & 7 != 6]
    rest[HALF_STRAIGHT] = lax.ppermute(kv_rest, "ctx", straight)
    rest[SIDE_ONWARD] = [rest[SIDE], lax.ppermute(rest[NEAR], "ctx", by_three)]
    late = far | {slot: fetched(kv_late, slot) for slot in (NEAR, SIDE, HALF)}
    far_blocks = BLOCKS - LATE
    state = local_part(info, queries, kv, LATE, far_blocks, 0)
    state = local_part(info, queries, kv, LATE, far_blocks, 1, state)
    late_state = local_part(info, queries, kv, 0, LATE)
    state = far_part(info, queries, state, rest, (NEAR, HALF_STRAIGHT, FOURTH, THIRD), LATE)
    sent = {}
    for some in (SWAPS[:2], SWAPS[2:]):
        sent |= zip(some, far_part(info, queries, state, rest, (SIDE_ONWARD,), LATE, some))
    late_state = far_part(info, queries, late_state, late, (FOURTH, THIRD), 0)
    parts = far_part(info, queries, late_state, late, (NEAR, SIDE, HALF), 0, range(LATE))
    parts += [sent[n] for n in range(LATE, BLOCKS)]
    parts = parts[:1] + [swapped(parts[n], n) for n in range(1, BLOCKS)]
    return norm_part(info, parts, residual, norm_gain.reshape(1, -1))


def solution(mesh):
    in_specs = (
        P("ctx", "head"),
        P("ctx", "head"),
        P("ctx", "head"),
        P("head", "ctx"),
        P(("ctx", "head"), None),
        P(),
    )
    out_specs = (P(("ctx", "head"), None), P(("ctx", "head"), None))
    return jax.shard_map(shards, mesh=mesh, in_specs=in_specs, out_specs=out_specs, check_vma=False)
```

```python
import functools

import jax
import jax.numpy as jnp
from jax import lax
from jax.experimental import pallas as pl
from jax.experimental.pallas import tpu as pltpu
from jax.sharding import PartitionSpec as P

DH = 128
BLOCK = 128
BLOCKS = 8
HEADS = 4
EPSILON = 1e-05
NEG = -1e30
KERNEL_VMEM = 16 * 2**20
SCALE = DH ** (-0.5) * 1.4426950408889634
LATE = 2
FIRST = 2
SWAPS = (4, 6, 3, 5, 7, 2)
EARLY = (0, 3, 4, 6)


NEAR, SIDE, HALF, FOURTH, THIRD = 1, 2, 3, 4, 5
SIDE_ONWARD, HALF_STRAIGHT = 6, 7


def slots(size):
    pairs = {slot: [] for slot in (NEAR, SIDE, HALF, FOURTH, THIRD)}
    for i in range(size):
        low = i & 3
        for slot, bit, taken in (
            (NEAR, 0, low == 3),
            (NEAR, 1, low == 2),
            (SIDE, 0, low == 1),
            (SIDE, 1, low == 3),
            (HALF, 2, i & 4),
            (THIRD, 3, i & 8),
            (FOURTH, 4, i & 16),
        ):
            if taken:
                pairs[slot].append((i - 2**bit, i))
    return pairs


def slot_level(slot, ctx, local_bits):
    bit = [lax.shift_right_logical(ctx, b) & 1 for b in range(5)]
    six = bit[2] & bit[1] & (1 - bit[0])
    taken, level = {
        SIDE_ONWARD: (bit[0] | six, jnp.where(six == 1, 2, bit[1])),
        HALF_STRAIGHT: (bit[2] & (1 - six), 2),
        NEAR: (bit[1], 1 - bit[0]),
        SIDE: (bit[0], bit[1]),
        HALF: (bit[2], 2),
        FOURTH: (bit[4], 4),
        THIRD: (bit[3], 3),
    }[slot]
    return jnp.where(taken == 1, local_bits + level, 31)


def held_in(space, *arrays):
    return [pltpu.with_memory_space_constraint(array, space) for array in arrays]


def params():
    return pltpu.CompilerParams(vmem_limit_bytes=KERNEL_VMEM)


def rows_at(index):
    return pl.ds(pl.multiple_of(index * BLOCK, BLOCK), BLOCK)


def in_vmem():
    return pl.BlockSpec(memory_space=pltpu.VMEM)


def order_kernel(info_ref, k_hbm, v_hbm, q_hbm, all_ref, late_ref, rest_ref, q_ref, k_ref, v_ref, sems):
    rank = info_ref[0, 0]
    copies = [pltpu.make_async_copy(k_hbm, k_ref, sems.at[0, 0]), pltpu.make_async_copy(v_hbm, v_ref, sems.at[0, 1])]
    for n in range(BLOCKS):
        for h in range(HEADS):
            source = q_hbm.at[rows_at(rank ^ n), h * DH : (h + 1) * DH]
            copies.append(
                pltpu.make_async_copy(source, q_ref.at[n, h * BLOCK : (h + 1) * BLOCK, :], sems.at[1 + n, h])
            )
    for copy in copies:
        copy.start()
    for copy in copies[:2]:
        copy.wait()
    for n in range(BLOCKS):
        source = rows_at(rank ^ n)
        key, val = k_ref[source, :], v_ref[source, :].T
        part, at = (late_ref, n) if n < LATE else (rest_ref, n - LATE)
        for ref, first in ((all_ref, n), (part, at)):
            ref[first * BLOCK : (first + 1) * BLOCK, :DH] = key
            ref[first * BLOCK : (first + 1) * BLOCK, DH:] = val
    for copy in copies[2:]:
        copy.wait()


def ordered(info, keys, values, queries):
    rows = keys.shape[0]
    hbm = pl.BlockSpec(memory_space=pl.ANY)
    return pl.pallas_call(
        order_kernel,
        in_specs=[pl.BlockSpec(memory_space=pltpu.SMEM), hbm, hbm, hbm],
        out_specs=[in_vmem()] * 4,
        out_shape=[
            jax.ShapeDtypeStruct((n, 2 * DH), jnp.bfloat16)
            for n in (rows, LATE * BLOCK, rows - LATE * BLOCK)
        ]
        + [jax.ShapeDtypeStruct((BLOCKS, HEADS * BLOCK, DH), jnp.bfloat16)],
        scratch_shapes=[pltpu.VMEM(keys.shape, jnp.bfloat16)] * 2 + [pltpu.SemaphoreType.DMA((1 + BLOCKS, HEADS))],
        compiler_params=params(),
        name="order",
    )(info, *held_in(pltpu.HBM, keys, values, queries))


def scores_of(q, keys):
    return lax.dot_general(
        jnp.concatenate(keys, 0), q, (((1,), (1,)), ((), ())), preferred_element_type=jnp.float32
    )


def staggered(items, *stages):
    items = list(items)
    values = {}
    for step in range(len(items) + len(stages) - 1):
        for number, stage in enumerate(stages):
            at = step - number
            if 0 <= at < len(items):
                values[at] = stage(items[at], *([values[at]] if number else []))


def weighted(scores, count, biases, causal=None, before=None):
    parts = [scores[n * BLOCK : (n + 1) * BLOCK, :] for n in range(count)]
    if causal is not None:
        parts[0] = jnp.where(causal, parts[0], NEG)
    tops = [part.max(0, keepdims=True) * SCALE + bias for part, bias in zip(parts, biases)]
    top = functools.reduce(jnp.maximum, tops if before is None else [before[0]] + tops)
    weights = [jnp.exp2(part * SCALE - (top - bias)) for part, bias in zip(parts, biases)]
    weight = jnp.concatenate([w.astype(jnp.bfloat16) for w in weights], 0)
    return weight, top, None if before is None else jnp.exp2(before[0] - top)


def summed_of(vals, weight):
    val = jnp.concatenate(vals, 1)
    val = jnp.concatenate([val, jnp.ones((16, val.shape[1]), jnp.bfloat16)], 0)
    summed = jnp.dot(val, weight, preferred_element_type=jnp.float32)
    return summed[:DH], summed[DH : DH + 1]


def bitmap_at(info_ref, h, j):
    return info_ref[1 + h, j]


def bias_of(bitmaps, level):
    pieces = []
    for bitmap in bitmaps:
        allowed = lax.shift_right_logical(bitmap, level) & 1
        pieces.append(jnp.full((1, BLOCK), (1 - allowed).astype(jnp.float32) * NEG))
    return jnp.concatenate(pieces, 1)


def local_kernel(first, count, turn, info_ref, q_ref, kv_ref, *refs):
    part_ref, stat_ref = refs[-2:]
    rank = info_ref[0, 0]

    def body():
        shape = (BLOCK, HEADS * BLOCK)
        causal = lax.broadcasted_iota(jnp.int32, shape, 0) <= (
            lax.broadcasted_iota(jnp.int32, shape, 1) & (BLOCK - 1)
        )
        levels = range(BLOCKS.bit_length() - 1)

        def blocks_of(i):
            n = first + i
            return [kv_ref[m * BLOCK : (m + 1) * BLOCK, :] for m in [n] + [n ^ 2**b for b in levels]]

        def start(i):
            return scores_of(q_ref[first + i], [kv[:, :DH] for kv in blocks_of(i)])

        def weigh(i, scores):
            j = rank ^ (first + i)
            bitmaps = [bitmap_at(info_ref, h, j) & j for h in range(HEADS)]
            biases = [0.0] + [bias_of(bitmaps, level) for level in levels]
            return weighted(scores, 1 + len(levels), biases, causal)

        def finish(i, found):
            weight, top, _ = found
            part_ref[i], total = summed_of([kv[:, DH:] for kv in blocks_of(i)], weight)
            stat_ref[i, 0:1, :] = top
            stat_ref[i, 1:2, :] = total

        staggered(range(count), start, weigh, finish)

    if turn is None:
        body()
    else:
        pl.when(((info_ref[0, 1] & 7) < FIRST) == (turn == 0))(body)


def local_part(info, queries, kv, first, count, turn=None, state=()):
    width = HEADS * DH
    return pl.pallas_call(
        functools.partial(local_kernel, first, count, turn),
        in_specs=[pl.BlockSpec(memory_space=pltpu.SMEM)] + [in_vmem()] * (2 + len(state)),
        out_specs=[in_vmem()] * 2,
        out_shape=[
            jax.ShapeDtypeStruct((count, DH, width), jnp.float32),
            jax.ShapeDtypeStruct((count, 8, width), jnp.float32),
        ],
        input_output_aliases={3 + n: n for n in range(len(state))},
        cost_estimate=pl.CostEstimate(
            flops=4 * 4 * count * BLOCK * width * BLOCK, bytes_accessed=4_000_000, transcendentals=4 * count * BLOCK * width
        ),
        compiler_params=params(),
        name="local",
    )(info, queries, kv, *state)


def far_kernel(held, first, count, final, info_ref, q_ref, part_ref, stat_ref, *refs):
    arrays = sum(number for _, number in held)
    kv_refs, outs = refs[:arrays], refs[arrays:]
    levels = [slot_level(slot, info_ref[0, 1], BLOCKS.bit_length() - 1) for slot, _ in held]
    blocks = [n - first for n in final] if final else range(count)

    def tiles_of(i, part):
        tiles, rest = [], kv_refs
        for _, number in held:
            pieces = []
            for ref in rest[:number]:
                at = (first + i if ref.shape[0] == BLOCKS * BLOCK else i) * BLOCK
                pieces.append(ref[at : at + BLOCK, part])
            rest = rest[number:]
            tiles.append(functools.reduce(jnp.add, pieces))
        return tiles

    def start(item):
        return scores_of(q_ref[first + item[1]], tiles_of(item[1], slice(0, DH)))

    def weigh(item, scores):
        _, i = item
        j = info_ref[0, 0] ^ (first + i)
        bitmaps = [bitmap_at(info_ref, h, j) for h in range(HEADS)]
        biases = [bias_of(bitmaps, level) for level in levels]
        return weighted(scores, len(levels), biases, None, (stat_ref[i, 0:1, :],))

    def finish(item, found):
        place, i = item
        weight, top, factor = found
        summed, total = summed_of(tiles_of(i, slice(DH, 2 * DH)), weight)
        summed = summed + part_ref[i] * factor
        total = total + stat_ref[i, 1:2, :] * factor
        if final:
            result = summed * (1.0 / total)
            for h in range(HEADS):
                at = slice(h * DH, (h + 1) * DH)
                outs[place][:, at] = result[:, at].T.astype(jnp.bfloat16)
        else:
            outs[0][i] = summed
            outs[1][i, 0:1, :] = top
            outs[1][i, 1:2, :] = total

    staggered(enumerate(blocks), start, weigh, finish)


def far_part(info, queries, state, fetched, held, first, final=()):
    part, stats = state
    count, _, width = part.shape
    kvs, numbers = [], []
    for slot in held:
        arrays = fetched[slot] if isinstance(fetched[slot], list) else [fetched[slot]]
        kvs += arrays
        numbers.append((slot, len(arrays)))
    if final:
        out_shape = [jax.ShapeDtypeStruct((BLOCK, width), jnp.bfloat16)] * len(final)
    else:
        out_shape = [
            jax.ShapeDtypeStruct((count, DH, width), jnp.float32),
            jax.ShapeDtypeStruct((count, 8, width), jnp.float32),
        ]
    outs = pl.pallas_call(
        functools.partial(far_kernel, numbers, first, count, final),
        in_specs=[pl.BlockSpec(memory_space=pltpu.SMEM)] + [in_vmem()] * (3 + len(kvs)),
        out_specs=[in_vmem()] * len(out_shape),
        out_shape=out_shape,
        cost_estimate=pl.CostEstimate(
            flops=len(kvs) * 4 * count * BLOCK * width * BLOCK,
            bytes_accessed=4_000_000,
            transcendentals=len(kvs) * count * BLOCK * width,
        ),
        compiler_params=params(),
        name="far",
    )(info, *held_in(pltpu.VMEM, queries, part, stats, *kvs))
    return list(outs)


def added(info_ref, n, part_ref, res_ref, stream_ref, stream_hbm, sem):
    width = part_ref.shape[1]
    cols = pl.ds(pl.multiple_of((info_ref[0, 0] ^ n) * width, width), width)
    summed = res_ref[:, cols].astype(jnp.float32) + part_ref[...].astype(jnp.float32)
    stream_ref[...] = summed.astype(jnp.bfloat16)
    copy = pltpu.make_async_copy(stream_ref, stream_hbm.at[:, cols], sem)
    copy.start()
    square = jnp.zeros((BLOCK, DH), jnp.float32)
    for c in range(0, width, DH):
        piece = summed[:, c : c + DH]
        square = square + piece * piece
    return summed, square, copy


def sums_kernel(groups, info_ref, *refs):
    parts = refs[: len(groups)]
    res_ref, stream_hbm, whole_ref, square_ref, stream_ref, sems = refs[len(groups) :]
    square = jnp.zeros((BLOCK, DH), jnp.float32)
    copies = []
    for i, n in enumerate(groups):
        summed, more, copy = added(info_ref, n, parts[i], res_ref, stream_ref.at[i], stream_hbm, sems.at[i])
        whole_ref[i] = summed
        square = square + more
        copies.append(copy)
    square_ref[...] = square
    for copy in copies:
        copy.wait()


def sums_part(info, groups, parts, residual):
    count, width = len(groups), parts[0].shape[1]
    return pl.pallas_call(
        functools.partial(sums_kernel, groups),
        in_specs=[pl.BlockSpec(memory_space=pltpu.SMEM)] + [in_vmem()] * (count + 1),
        out_specs=[pl.BlockSpec(memory_space=pl.ANY), in_vmem(), in_vmem()],
        out_shape=[
            jax.ShapeDtypeStruct(residual.shape, jnp.bfloat16),
            jax.ShapeDtypeStruct((count, BLOCK, width), jnp.float32),
            jax.ShapeDtypeStruct((BLOCK, DH), jnp.float32),
        ],
        scratch_shapes=[pltpu.VMEM((count, BLOCK, width), jnp.bfloat16), pltpu.SemaphoreType.DMA((count,))],
        cost_estimate=pl.CostEstimate(flops=2_000_000, bytes_accessed=2_000_000, transcendentals=0),
        compiler_params=params(),
        name="sums",
    )(info, *held_in(pltpu.VMEM, *parts), residual)


def norm_kernel(groups, before, info_ref, *refs):
    parts = refs[: len(groups)]
    res_ref, gain_ref, _, held_ref, square_ref, stream_hbm, normed_hbm = refs[len(groups) : len(groups) + 7]
    whole, stream_ref, normed_ref, sems = refs[len(groups) + 7 :]
    width = parts[0].shape[1]
    square = square_ref[...]
    copies = []
    for i, n in enumerate(groups):
        summed, more, copy = added(info_ref, n, parts[i], res_ref, stream_ref.at[i], stream_hbm, sems.at[0, n])
        whole[i] = summed
        square = square + more
        copies.append(copy)
    mean = square.sum(-1, keepdims=True) / (BLOCKS * width)
    factor = lax.rsqrt(mean + EPSILON)
    for n in range(BLOCKS):
        cols = pl.ds(pl.multiple_of((info_ref[0, 0] ^ n) * width, width), width)
        summed = held_ref[before.index(n)] if n in before else whole[groups.index(n)]
        normed_ref[n] = (summed * factor * gain_ref[:, cols].astype(jnp.float32)).astype(jnp.bfloat16)
        copies.append(pltpu.make_async_copy(normed_ref.at[n], normed_hbm.at[:, cols], sems.at[1, n]))
        copies[-1].start()
    for copy in copies:
        copy.wait()


def norm_part(info, groups, parts, before, held, residual, gain):
    count, width = len(groups), parts[0].shape[1]
    stream, whole, square = held
    hbm = pl.BlockSpec(memory_space=pl.ANY)
    return pl.pallas_call(
        functools.partial(norm_kernel, groups, before),
        in_specs=[pl.BlockSpec(memory_space=pltpu.SMEM)] + [in_vmem()] * (count + 2) + [hbm] + [in_vmem()] * 2,
        out_specs=[hbm] * 2,
        out_shape=[jax.ShapeDtypeStruct(residual.shape, jnp.bfloat16)] * 2,
        scratch_shapes=[
            pltpu.VMEM((count, BLOCK, width), jnp.float32),
            pltpu.VMEM((count, BLOCK, width), jnp.bfloat16),
            pltpu.VMEM((BLOCKS, BLOCK, width), jnp.bfloat16),
            pltpu.SemaphoreType.DMA((2, BLOCKS)),
        ],
        input_output_aliases={3 + count: 0},
        cost_estimate=pl.CostEstimate(flops=4_000_000, bytes_accessed=4_000_000, transcendentals=128),
        compiler_params=params(),
        name="norm",
    )(info, *held_in(pltpu.VMEM, *parts), residual, gain, stream, *held_in(pltpu.VMEM, whole, square))


def shards(queries, keys, values, block_masks, residual, norm_gain):
    groups = lax.axis_size("head")
    routes = slots(lax.axis_size("ctx"))
    at = lax.broadcasted_iota(jnp.int32, (1, BLOCKS), 1)
    place = jnp.where(at == 0, lax.axis_index("head"), lax.axis_index("ctx")).astype(jnp.int32)
    info = jnp.concatenate([place, block_masks], 0)

    def fetched(array, slot):
        return lax.ppermute(array, "ctx", routes[slot])

    def swapped(array, n):
        return lax.ppermute(array, "head", [(i, i ^ n) for i in range(groups)])

    by_three = [(i - 3, i) for i in range(lax.axis_size("ctx")) if i & 7 == 6]

    kv, kv_late, kv_rest, queries = ordered(info, keys, values, queries)
    far = {slot: fetched(kv, slot) for slot in (FOURTH, THIRD)}
    rest = far | {slot: fetched(kv_rest, slot) for slot in (NEAR, SIDE)}
    straight = [(i, j) for i, j in routes[HALF] if j & 7 != 6]
    rest[HALF_STRAIGHT] = lax.ppermute(kv_rest, "ctx", straight)
    rest[SIDE_ONWARD] = [rest[SIDE], lax.ppermute(rest[NEAR], "ctx", by_three)]
    late = far | {slot: fetched(kv_late, slot) for slot in (NEAR, SIDE, HALF)}
    far_blocks = BLOCKS - LATE
    state = local_part(info, queries, kv, LATE, far_blocks, 0)
    state = local_part(info, queries, kv, LATE, far_blocks, 1, state)
    late_state = local_part(info, queries, kv, 0, LATE)
    state = far_part(info, queries, state, rest, (NEAR, FOURTH, THIRD), LATE)
    sent = {}
    for some in (SWAPS[:4], SWAPS[4:]):
        sent |= zip(some, far_part(info, queries, state, rest, (SIDE_ONWARD, HALF_STRAIGHT), LATE, some))
    late_state = far_part(info, queries, late_state, late, (FOURTH, THIRD), 0)
    parts = far_part(info, queries, late_state, late, (NEAR, SIDE, HALF), 0, range(LATE))
    parts += [sent[n] for n in range(LATE, BLOCKS)]
    parts = parts[:1] + [swapped(parts[n], n) for n in range(1, BLOCKS)]
    soon = [n for n in range(BLOCKS) if n in EARLY]
    last = [n for n in range(BLOCKS) if n not in EARLY]
    held = sums_part(info, soon, [parts[n] for n in soon], residual)
    gain = norm_gain.reshape(1, -1)
    return norm_part(info, last, [parts[n] for n in last], soon, held, residual, gain)


def solution(mesh):
    in_specs = (
        P("ctx", "head"),
        P("ctx", "head"),
        P("ctx", "head"),
        P("head", "ctx"),
        P(("ctx", "head"), None),
        P(),
    )
    out_specs = (P(("ctx", "head"), None), P(("ctx", "head"), None))
    return jax.shard_map(shards, mesh=mesh, in_specs=in_specs, out_specs=out_specs, check_vma=False)
```

```python
import functools

import jax
import jax.numpy as jnp
from jax import lax
from jax.experimental import pallas as pl
from jax.experimental.pallas import tpu as pltpu
from jax.sharding import PartitionSpec as P

DH = 128
BLOCK = 128
BLOCKS = 8
HEADS = 4
EPSILON = 1e-05
NEG = -1e30
KERNEL_VMEM = 16 * 2**20
SCALE = DH ** (-0.5) * 1.4426950408889634
LATE = 2
FIRST = 2
SWAPS = (4, 6, 3, 5, 7, 2)
EARLY = (0, 1, 3, 4, 6)


NEAR, SIDE, HALF, FOURTH, THIRD = 1, 2, 3, 4, 5
SIDE_ONWARD, HALF_STRAIGHT = 6, 7


def slots(size):
    pairs = {slot: [] for slot in (NEAR, SIDE, HALF, FOURTH, THIRD)}
    for i in range(size):
        low = i & 3
        for slot, bit, taken in (
            (NEAR, 0, low == 3),
            (NEAR, 1, low == 2),
            (SIDE, 0, low == 1),
            (SIDE, 1, low == 3),
            (HALF, 2, i & 4),
            (THIRD, 3, i & 8),
            (FOURTH, 4, i & 16),
        ):
            if taken:
                pairs[slot].append((i - 2**bit, i))
    return pairs


def slot_level(slot, ctx, local_bits):
    bit = [lax.shift_right_logical(ctx, b) & 1 for b in range(5)]
    six = bit[2] & bit[1] & (1 - bit[0])
    taken, level = {
        SIDE_ONWARD: (bit[0] | six, jnp.where(six == 1, 2, bit[1])),
        HALF_STRAIGHT: (bit[2] & (1 - six), 2),
        NEAR: (bit[1], 1 - bit[0]),
        SIDE: (bit[0], bit[1]),
        HALF: (bit[2], 2),
        FOURTH: (bit[4], 4),
        THIRD: (bit[3], 3),
    }[slot]
    return jnp.where(taken == 1, local_bits + level, 31)


def held_in(space, *arrays):
    return [pltpu.with_memory_space_constraint(array, space) for array in arrays]


def params():
    return pltpu.CompilerParams(vmem_limit_bytes=KERNEL_VMEM)


def rows_at(index):
    return pl.ds(pl.multiple_of(index * BLOCK, BLOCK), BLOCK)


def in_vmem():
    return pl.BlockSpec(memory_space=pltpu.VMEM)


def order_kernel(info_ref, k_hbm, v_hbm, q_hbm, all_ref, late_ref, rest_ref, q_ref, k_ref, v_ref, sems):
    rank = info_ref[0, 0]
    copies = [pltpu.make_async_copy(k_hbm, k_ref, sems.at[0]), pltpu.make_async_copy(v_hbm, v_ref, sems.at[1])]
    for n in range(BLOCKS):
        copies.append(pltpu.make_async_copy(q_hbm.at[rows_at(rank ^ n), :], q_ref.at[n], sems.at[2 + n]))
    for copy in copies:
        copy.start()
    for copy in copies[:2]:
        copy.wait()
    for n in range(BLOCKS):
        source = rows_at(rank ^ n)
        key, val = k_ref[source, :], v_ref[source, :].T
        part, at = (late_ref, n) if n < LATE else (rest_ref, n - LATE)
        for ref, first in ((all_ref, n), (part, at)):
            ref[first * BLOCK : (first + 1) * BLOCK, :DH] = key
            ref[first * BLOCK : (first + 1) * BLOCK, DH:] = val
    for copy in copies[2:]:
        copy.wait()


def ordered(place, keys, values, queries):
    rows = keys.shape[0]
    hbm = pl.BlockSpec(memory_space=pl.ANY)
    return pl.pallas_call(
        order_kernel,
        in_specs=[pl.BlockSpec(memory_space=pltpu.SMEM), hbm, hbm, hbm],
        out_specs=[in_vmem()] * 4,
        out_shape=[
            jax.ShapeDtypeStruct((n, 2 * DH), jnp.bfloat16)
            for n in (rows, LATE * BLOCK, rows - LATE * BLOCK)
        ]
        + [jax.ShapeDtypeStruct((BLOCKS, BLOCK, HEADS * DH), jnp.bfloat16)],
        scratch_shapes=[pltpu.VMEM(keys.shape, jnp.bfloat16)] * 2 + [pltpu.SemaphoreType.DMA((2 + BLOCKS,))],
        compiler_params=params(),
        name="order",
    )(place, *held_in(pltpu.HBM, keys, values, queries))


def scores_of(q, keys):
    q = jnp.concatenate([q[:, h * DH : (h + 1) * DH] for h in range(HEADS)], 0)
    return lax.dot_general(
        jnp.concatenate(keys, 0), q, (((1,), (1,)), ((), ())), preferred_element_type=jnp.float32
    )


def staggered(items, *stages):
    items = list(items)
    values = {}
    for step in range(len(items) + len(stages) - 1):
        for number, stage in enumerate(stages):
            at = step - number
            if 0 <= at < len(items):
                values[at] = stage(items[at], *([values[at]] if number else []))


def weighted(scores, count, biases, causal=None, before=None):
    parts = [scores[n * BLOCK : (n + 1) * BLOCK, :] for n in range(count)]
    if causal is not None:
        parts[0] = jnp.where(causal, parts[0], NEG)
    tops = [part.max(0, keepdims=True) * SCALE + bias for part, bias in zip(parts, biases)]
    top = functools.reduce(jnp.maximum, tops if before is None else [before[0]] + tops)
    weights = [jnp.exp2(part * SCALE - (top - bias)) for part, bias in zip(parts, biases)]
    weight = jnp.concatenate([w.astype(jnp.bfloat16) for w in weights], 0)
    return weight, top, None if before is None else jnp.exp2(before[0] - top)


def summed_of(vals, weight):
    val = jnp.concatenate(vals, 1)
    val = jnp.concatenate([val, jnp.ones((16, val.shape[1]), jnp.bfloat16)], 0)
    summed = jnp.dot(val, weight, preferred_element_type=jnp.float32)
    return summed[:DH], summed[DH : DH + 1]


def bitmap_at(info_ref, h, j):
    return info_ref[1 + h, j]


def bias_of(bitmaps, level):
    pieces = []
    for bitmap in bitmaps:
        allowed = lax.shift_right_logical(bitmap, level) & 1
        pieces.append(jnp.full((1, BLOCK), (1 - allowed).astype(jnp.float32) * NEG))
    return jnp.concatenate(pieces, 1)


def local_kernel(turn, info_ref, q_ref, kv_ref, *refs):
    part_ref, stat_ref = refs[-2:]
    rank = info_ref[0, 0]

    def body():
        shape = (BLOCK, HEADS * BLOCK)
        causal = lax.broadcasted_iota(jnp.int32, shape, 0) <= (
            lax.broadcasted_iota(jnp.int32, shape, 1) & (BLOCK - 1)
        )
        levels = range(BLOCKS.bit_length() - 1)

        def blocks_of(n):
            return [kv_ref[m * BLOCK : (m + 1) * BLOCK, :] for m in [n] + [n ^ 2**b for b in levels]]

        def start(i):
            return scores_of(q_ref[i], [kv[:, :DH] for kv in blocks_of(i)])

        def weigh(i, scores):
            j = rank ^ i
            bitmaps = [bitmap_at(info_ref, h, j) & j for h in range(HEADS)]
            biases = [0.0] + [bias_of(bitmaps, level) for level in levels]
            return weighted(scores, 1 + len(levels), biases, causal)

        def finish(i, found):
            weight, top, _ = found
            part_ref[i], total = summed_of([kv[:, DH:] for kv in blocks_of(i)], weight)
            stat_ref[i, 0:1, :] = top
            stat_ref[i, 1:2, :] = total

        staggered(range(BLOCKS), start, weigh, finish)

    pl.when(((info_ref[0, 1] & 7) < FIRST) == (turn == 0))(body)


def local_part(info, queries, kv, turn, state=()):
    count, width = BLOCKS, HEADS * DH
    return pl.pallas_call(
        functools.partial(local_kernel, turn),
        in_specs=[pl.BlockSpec(memory_space=pltpu.SMEM)] + [in_vmem()] * (2 + len(state)),
        out_specs=[in_vmem()] * 2,
        out_shape=[
            jax.ShapeDtypeStruct((count, DH, width), jnp.float32),
            jax.ShapeDtypeStruct((count, 8, width), jnp.float32),
        ],
        input_output_aliases={3 + n: n for n in range(len(state))},
        cost_estimate=pl.CostEstimate(
            flops=4 * 4 * count * BLOCK * width * BLOCK, bytes_accessed=4_000_000, transcendentals=4 * count * BLOCK * width
        ),
        compiler_params=params(),
        name="local",
    )(info, queries, kv, *state)


def far_kernel(held, first, count, final, info_ref, q_ref, part_ref, stat_ref, *refs):
    arrays = sum(number for _, number in held)
    kv_refs, outs = refs[:arrays], refs[arrays:]
    levels = [slot_level(slot, info_ref[0, 1], BLOCKS.bit_length() - 1) for slot, _ in held]
    base = first if part_ref.shape[0] == BLOCKS else 0
    blocks = [n - first for n in final] if final else range(count)

    def tiles_of(i, part):
        tiles, rest = [], kv_refs
        for _, number in held:
            pieces = []
            for ref in rest[:number]:
                at = (first + i if ref.shape[0] == BLOCKS * BLOCK else i) * BLOCK
                pieces.append(ref[at : at + BLOCK, part])
            rest = rest[number:]
            tiles.append(functools.reduce(jnp.add, pieces))
        return tiles

    def start(item):
        return scores_of(q_ref[first + item[1]], tiles_of(item[1], slice(0, DH)))

    def weigh(item, scores):
        _, i = item
        j = info_ref[0, 0] ^ (first + i)
        bitmaps = [bitmap_at(info_ref, h, j) for h in range(HEADS)]
        biases = [bias_of(bitmaps, level) for level in levels]
        return weighted(scores, len(levels), biases, None, (stat_ref[base + i, 0:1, :],))

    def finish(item, found):
        place, i = item
        weight, top, factor = found
        summed, total = summed_of(tiles_of(i, slice(DH, 2 * DH)), weight)
        summed = summed + part_ref[base + i] * factor
        total = total + stat_ref[base + i, 1:2, :] * factor
        if final:
            result = summed * (1.0 / total)
            for h in range(HEADS):
                at = slice(h * DH, (h + 1) * DH)
                outs[place][:, at] = result[:, at].T.astype(jnp.bfloat16)
        else:
            outs[0][i] = summed
            outs[1][i, 0:1, :] = top
            outs[1][i, 1:2, :] = total

    staggered(enumerate(blocks), start, weigh, finish)


def far_part(info, queries, state, fetched, held, first, final=()):
    part, stats = state
    count, width = BLOCKS - LATE if first else LATE, part.shape[2]
    kvs, numbers = [], []
    for slot in held:
        arrays = fetched[slot] if isinstance(fetched[slot], list) else [fetched[slot]]
        kvs += arrays
        numbers.append((slot, len(arrays)))
    if final:
        out_shape = [jax.ShapeDtypeStruct((BLOCK, width), jnp.bfloat16)] * len(final)
    else:
        out_shape = [
            jax.ShapeDtypeStruct((count, DH, width), jnp.float32),
            jax.ShapeDtypeStruct((count, 8, width), jnp.float32),
        ]
    outs = pl.pallas_call(
        functools.partial(far_kernel, numbers, first, count, final),
        in_specs=[pl.BlockSpec(memory_space=pltpu.SMEM)] + [in_vmem()] * (3 + len(kvs)),
        out_specs=[in_vmem()] * len(out_shape),
        out_shape=out_shape,
        cost_estimate=pl.CostEstimate(
            flops=len(kvs) * 4 * count * BLOCK * width * BLOCK,
            bytes_accessed=4_000_000,
            transcendentals=len(kvs) * count * BLOCK * width,
        ),
        compiler_params=params(),
        name="far",
    )(info, *held_in(pltpu.VMEM, queries, part, stats, *kvs))
    return list(outs)


def added(info_ref, n, part_ref, res_ref, stream_ref, stream_hbm, sem):
    width = part_ref.shape[1]
    cols = pl.ds(pl.multiple_of((info_ref[0, 0] ^ n) * width, width), width)
    summed = res_ref[:, cols].astype(jnp.float32) + part_ref[...].astype(jnp.float32)
    stream_ref[...] = summed.astype(jnp.bfloat16)
    copy = pltpu.make_async_copy(stream_ref, stream_hbm.at[:, cols], sem)
    copy.start()
    square = jnp.zeros((BLOCK, DH), jnp.float32)
    for c in range(0, width, DH):
        piece = summed[:, c : c + DH]
        square = square + piece * piece
    return summed, square, copy


def sums_kernel(groups, info_ref, *refs):
    parts = refs[: len(groups)]
    res_ref, stream_hbm, whole_ref, square_ref, stream_ref, sems = refs[len(groups) :]
    square = jnp.zeros((BLOCK, DH), jnp.float32)
    copies = []
    for i, n in enumerate(groups):
        summed, more, copy = added(info_ref, n, parts[i], res_ref, stream_ref.at[i], stream_hbm, sems.at[i])
        whole_ref[i] = summed
        square = square + more
        copies.append(copy)
    square_ref[...] = square
    for copy in copies:
        copy.wait()


def sums_part(info, groups, parts, residual):
    count, width = len(groups), parts[0].shape[1]
    return pl.pallas_call(
        functools.partial(sums_kernel, groups),
        in_specs=[pl.BlockSpec(memory_space=pltpu.SMEM)] + [in_vmem()] * (count + 1),
        out_specs=[pl.BlockSpec(memory_space=pl.ANY), in_vmem(), in_vmem()],
        out_shape=[
            jax.ShapeDtypeStruct(residual.shape, jnp.bfloat16),
            jax.ShapeDtypeStruct((count, BLOCK, width), jnp.float32),
            jax.ShapeDtypeStruct((BLOCK, DH), jnp.float32),
        ],
        scratch_shapes=[pltpu.VMEM((count, BLOCK, width), jnp.bfloat16), pltpu.SemaphoreType.DMA((count,))],
        cost_estimate=pl.CostEstimate(flops=2_000_000, bytes_accessed=2_000_000, transcendentals=0),
        compiler_params=params(),
        name="sums",
    )(info, *held_in(pltpu.VMEM, *parts), residual)


def norm_kernel(groups, before, info_ref, *refs):
    parts = refs[: len(groups)]
    res_ref, gain_ref, _, held_ref, square_ref, stream_hbm, normed_hbm = refs[len(groups) : len(groups) + 7]
    whole, stream_ref, normed_ref, sems = refs[len(groups) + 7 :]
    width = parts[0].shape[1]
    square = square_ref[...]
    copies = []
    for i, n in enumerate(groups):
        summed, more, copy = added(info_ref, n, parts[i], res_ref, stream_ref.at[i], stream_hbm, sems.at[0, n])
        whole[i] = summed
        square = square + more
        copies.append(copy)
    mean = square.sum(-1, keepdims=True) / (BLOCKS * width)
    factor = lax.rsqrt(mean + EPSILON)
    for n in range(BLOCKS):
        cols = pl.ds(pl.multiple_of((info_ref[0, 0] ^ n) * width, width), width)
        summed = held_ref[before.index(n)] if n in before else whole[groups.index(n)]
        normed_ref[n] = (summed * factor * gain_ref[:, cols].astype(jnp.float32)).astype(jnp.bfloat16)
        copies.append(pltpu.make_async_copy(normed_ref.at[n], normed_hbm.at[:, cols], sems.at[1, n]))
        copies[-1].start()
    for copy in copies:
        copy.wait()


def norm_part(info, groups, parts, before, held, residual, gain):
    count, width = len(groups), parts[0].shape[1]
    stream, whole, square = held
    hbm = pl.BlockSpec(memory_space=pl.ANY)
    return pl.pallas_call(
        functools.partial(norm_kernel, groups, before),
        in_specs=[pl.BlockSpec(memory_space=pltpu.SMEM)] + [in_vmem()] * (count + 2) + [hbm] + [in_vmem()] * 2,
        out_specs=[hbm] * 2,
        out_shape=[jax.ShapeDtypeStruct(residual.shape, jnp.bfloat16)] * 2,
        scratch_shapes=[
            pltpu.VMEM((count, BLOCK, width), jnp.float32),
            pltpu.VMEM((count, BLOCK, width), jnp.bfloat16),
            pltpu.VMEM((BLOCKS, BLOCK, width), jnp.bfloat16),
            pltpu.SemaphoreType.DMA((2, BLOCKS)),
        ],
        input_output_aliases={3 + count: 0},
        cost_estimate=pl.CostEstimate(flops=4_000_000, bytes_accessed=4_000_000, transcendentals=128),
        compiler_params=params(),
        name="norm",
    )(info, *held_in(pltpu.VMEM, *parts), residual, gain, stream, *held_in(pltpu.VMEM, whole, square))


def shards(queries, keys, values, block_masks, residual, norm_gain):
    groups = lax.axis_size("head")
    routes = slots(lax.axis_size("ctx"))
    at = lax.broadcasted_iota(jnp.int32, (1, BLOCKS), 1)
    place = jnp.where(at == 0, lax.axis_index("head"), lax.axis_index("ctx")).astype(jnp.int32)
    info = jnp.concatenate([place, block_masks], 0)

    def fetched(array, slot):
        return lax.ppermute(array, "ctx", routes[slot])

    def swapped(array, n):
        return lax.ppermute(array, "head", [(i, i ^ n) for i in range(groups)])

    by_three = [(i - 3, i) for i in range(lax.axis_size("ctx")) if i & 7 == 6]

    kv, kv_late, kv_rest, queries = ordered(place, keys, values, queries)
    far = {slot: fetched(kv, slot) for slot in (FOURTH, THIRD)}
    rest = far | {slot: fetched(kv_rest, slot) for slot in (NEAR, SIDE)}
    some = [(i, j) for i, j in routes[HALF] if j & 7 in (4, 5)]
    rest[HALF_STRAIGHT] = [lax.ppermute(kv_rest, "ctx", some)]
    some = [(i, j) for i, j in routes[HALF] if j & 7 == 7]
    rest[HALF_STRAIGHT] += [lax.ppermute(kv_rest, "ctx", some)]
    rest[SIDE_ONWARD] = [rest[SIDE], lax.ppermute(rest[NEAR], "ctx", by_three)]
    late = far | {slot: fetched(kv_late, slot) for slot in (NEAR, SIDE, HALF)}
    own = local_part(info, queries, kv, 0)
    own = local_part(info, queries, kv, 1, own)
    state = far_part(info, queries, own, rest, (NEAR, FOURTH), LATE)
    state = far_part(info, queries, state, rest, (THIRD,), LATE)
    sent = {}
    for some in (SWAPS,):
        sent |= zip(some, far_part(info, queries, state, rest, (SIDE_ONWARD, HALF_STRAIGHT), LATE, some))
    parts = far_part(info, queries, own, late, (FOURTH, THIRD, NEAR, SIDE, HALF), 0, range(LATE))
    parts += [sent[n] for n in range(LATE, BLOCKS)]
    parts = parts[:1] + [swapped(parts[n], n) for n in range(1, BLOCKS)]
    soon = [n for n in range(BLOCKS) if n in EARLY]
    last = [n for n in range(BLOCKS) if n not in EARLY]
    held = sums_part(info, soon, [parts[n] for n in soon], residual)
    gain = norm_gain.reshape(1, -1)
    return norm_part(info, last, [parts[n] for n in last], soon, held, residual, gain)


def solution(mesh):
    in_specs = (
        P("ctx", "head"),
        P("ctx", "head"),
        P("ctx", "head"),
        P("head", "ctx"),
        P(("ctx", "head"), None),
        P(),
    )
    out_specs = (P(("ctx", "head"), None), P(("ctx", "head"), None))
    return jax.shard_map(shards, mesh=mesh, in_specs=in_specs, out_specs=out_specs, check_vma=False)
```
